128 devices in a mesh: row: 16 (over z_hi, y, core), col: 8 (over z_lo, x).
Axes of the slice: x: 4, y: 4, z: 4 (z_hi: 2, z_lo: 2; z = z_hi * 2 + z_lo), core: 2. Of those that a mesh axis runs over, the one named last changes fastest.
Arguments:
- parent_inverse: float32 [24576, 24576], P('row', 'col'), may hold values from -6 to 6
- panel: float32 [24576, 1024], P(('col', 'row')), may hold values from -0.0390625 to 0.0390625
- saved_diag: float32 [1024, 1024], P('row', 'col'), may hold values from -6 to 6
Outputs:
- offdiag_block: float32 [24576, 1024], P(('row', 'col'))
- diag_block: float32 [1024, 1024], P('row', 'col')
The draws below stay inside these ranges and needn't reach their ends.
All inputs are finite; a program needn't handle non-finite values.
Results may differ from the reference program's by a relative error of at most 0.00007.
Values sent between devices are 32-bit elements; how exact they have to be, the bound alone decides.
A program may use at most 128 MiB of HBM per device.

```python
import jax
import jax.numpy as jnp
from jax import lax

B = 24576
P_SIZE = 1024


def block_scale(rng, shape, pieces, smallest, largest):
    def one(position, parts):
        heights = jax.random.uniform(jax.random.fold_in(jax.random.fold_in(rng, 6), position), (parts,), jnp.float32, smallest / len(pieces), largest / len(pieces))
        return jnp.repeat(jnp.exp(heights), shape[position] // parts).reshape((-1,) + (1,) * (len(shape) - position - 1))

    level = one(*pieces[0])
    for cut in pieces[1:]:
        level = level * one(*cut)
    return level


def gaussian(rng, extent, spread, bound, split=(), dtype=jnp.bfloat16):
    drawn = spread * jax.random.normal(rng, extent, jnp.float32)
    if split:
        drawn = drawn * block_scale(rng, extent, split, -0.22, 0.18)
    return jnp.clip(drawn, -bound, bound).astype(dtype)


def setup_inputs(seed: int = 0) -> dict:
    seeds = jax.random.split(jax.random.key(seed), 4)
    return {
        "parent_inverse": gaussian(seeds[0], (B, B), 1.0, 6.0, ((0, 16), (1, 8)), jnp.float32),
        "panel": gaussian(seeds[1], (B, P_SIZE), B ** -0.5, 0.0390625, ((0, 128),), jnp.float32),
        "saved_diag": gaussian(seeds[2], (P_SIZE, P_SIZE), 1.0, 6.0, ((0, 16), (1, 8)), jnp.float32),
    }


def reference(parent_inverse, panel, saved_diag):
    product = jnp.dot(parent_inverse, panel, precision=lax.Precision.HIGHEST, preferred_element_type=jnp.float32)
    offdiag_block = -product
    gram = jnp.dot(panel.T, product, precision=lax.Precision.HIGHEST, preferred_element_type=jnp.float32)
    diag_block = saved_diag + gram
    return offdiag_block, diag_block
```

```python
import jax
import jax.numpy as jnp
from jax import lax
from jax.experimental import pallas as pl
from jax.experimental.pallas import tpu as pltpu
from jax.sharding import PartitionSpec as P

MESH = pl.DeviceIdType.MESH
F32 = jnp.float32
BF16 = jnp.bfloat16
J = 4
W = 256
H = 128
R = 192
K = 3072
SLABS = K // W


def dot(a, b):
    return jnp.dot(a, b, preferred_element_type=F32)


def split(value):
    high = value.astype(BF16)
    return high, (value - high.astype(F32)).astype(BF16)


def kernel(
    pi, panel, saved, out, diag,
    pih, pil, gath, bh, bl, relay, x1r, x2f, x2b, zrec, part, rows, pth, ptl, gp, gsr, a2a, fin, fsend,
    pisem, locsem, ag_s, ag_r, rs_s, rs_r, g_s, g_r, a_s, a_r, f_s, f_r, p_s, p_r,
):
    r, c = lax.axis_index("row"), lax.axis_index("col")
    zh, y, k = r // 8, (r // 2) % 4, r % 2
    zl, x = c // 4, c % 4
    z = zh * 2 + zl
    d = 1 - 2 * k

    def dev(z_, y_, x_, k_):
        return ((z_ // 2) * 8 + y_ * 2 + k_, (z_ % 2) * 4 + x_)

    def slot(zh_, y_, k_):
        return zh_ * 8 + y_ * 2 + k_

    yf, yb, y2 = (y + d + 4) % 4, (y - d + 4) % 4, (y + 2) % 4
    zf, zb = (z + d + 4) % 4, (z - d + 4) % 4
    xf, xb, x2 = (x + d + 4) % 4, (x - d + 4) % 4, (x + 2) % 4
    zp = zh * 2 + (1 - zl)
    zo = 1 - zh
    sib = dev(z, y, x, 1 - k)
    to_yf, to_yb = dev(z, yf, x, k), dev(z, yb, x, k)
    to_zf, to_zp = dev(zf, y, x, k), dev(zp, y, x, k)
    to_xf, to_xb = dev(z, y, xf, k), dev(z, y, xb, k)
    perm_to = (2 * c + r // 8, r % 8)
    perm_block = 8 * r + c
    perm_from = (perm_block % 16, perm_block // 16)
    moves = jnp.logical_or(perm_to[0] != r, perm_to[1] != c)

    def remote(src, dst, ss, rs, to):
        return pltpu.make_async_remote_copy(
            src_ref=src, dst_ref=dst, send_sem=ss, recv_sem=rs, device_id=to, device_id_type=MESH
        )

    def own_copy(j, h):
        return pltpu.make_async_copy(
            panel.at[:, pl.ds(h * 512 + j * H, H)], gath.at[j, r, :, pl.ds(h * H, H)], locsem.at[j, h]
        )

    def slab_copy(s, b):
        return pltpu.make_async_copy(
            pi.at[:, :, pl.ds(pl.multiple_of(s * W, W), W)], part.at[b], pisem.at[b]
        )

    for j in range(J):
        for h in range(2):
            own_copy(j, h).start()
    for b in range(4):
        slab_copy(b, b).start()

    barrier = pltpu.get_barrier_semaphore()

    def greet(to):
        pl.semaphore_signal(barrier, inc=1, device_id=to, device_id_type=MESH)

    def greet_plane(i, carry):
        greet(dev((z + i // 4) % 4, (y + i % 4) % 4, x, k))
        return carry

    lax.fori_loop(1, 16, greet_plane, 0)
    greet(sib)
    for dx in range(1, 4):
        greet(dev(z, y, (x + dx) % 4, k))

    @pl.when(moves)
    def _():
        greet(perm_to)
        greet(perm_from)

    pl.semaphore_wait(barrier, jnp.where(moves, 21, 19))

    sib_slots = [slot(zh, y, k), slot(zh, yb, k), slot(zh, yf, k), slot(zo, y, k),
                 slot(zh, y2, k), slot(zo, yb, k), slot(zo, yf, k), slot(zo, y2, k)]
    from_sib = [slot(zh, y, 1 - k), slot(zh, yf, 1 - k), slot(zh, yb, 1 - k), slot(zo, y, 1 - k),
                slot(zh, y2, 1 - k), slot(zo, yf, 1 - k), slot(zo, yb, 1 - k), slot(zo, y2, 1 - k)]
    got = [slot(zh, yb, k), slot(zh, yf, k), None, slot(zo, y, k), slot(zo, yb, k), slot(zo, yf, k),
           slot(zh, y2, k), slot(zo, y2, k)]
    relay_slot = slot(zb // 2, y, k)

    def ag(j, m):
        ss, rs = ag_s.at[j, m], ag_r.at[j, m]
        if m == 2:
            return remote(gath.at[j, r], relay.at[j], ss, rs, to_zf)
        if m == 3:
            return remote(relay.at[j], gath.at[j, relay_slot], ss, rs, to_zf)
        if m >= 8:
            at = gath.at[j, sib_slots[m - 8]]
            return remote(at, at, ss, rs, sib)
        source = {0: r, 1: r, 4: got[3], 5: got[3], 6: got[0], 7: got[4]}[m]
        at = gath.at[j, source]
        return remote(at, at, ss, rs, to_yb if m in (1, 5) else to_yf)

    def ag_wait(j, m):
        if m == 2:
            at = relay.at[j]
        elif m >= 8:
            at = gath.at[j, from_sib[m - 8]]
        else:
            at = gath.at[j, got[m]]
        remote(at, at, ag_s.at[j, m], ag_r.at[j, m], sib).wait_recv()

    def p0(j):
        for h in range(2):
            own_copy(j, h).wait()
        for m in (0, 2, 1, 8):
            ag(j, m).start()

    def p1(j):
        ag_wait(j, 2)
        ag(j, 3).start()
        ag_wait(j, 0)
        ag(j, 6).start()
        ag(j, 9).start()
        ag_wait(j, 1)
        ag(j, 10).start()

    def p2(j):
        ag_wait(j, 3)
        ag(j, 4).start()
        ag(j, 5).start()
        ag(j, 11).start()
        ag_wait(j, 6)
        ag(j, 12).start()

    def p3(j):
        ag_wait(j, 4)
        ag(j, 7).start()
        ag(j, 13).start()
        ag_wait(j, 5)
        ag(j, 14).start()

    def p4(j):
        ag_wait(j, 7)
        ag(j, 15).start()

    def p5(j):
        for m in range(8, 16):
            ag_wait(j, m)

    def split_slabs(first, last):
        def body(s, carry):
            b = s % 4
            slab_copy(s, b).wait()

            def piece(q, carry):
                high, low = split(part[b, q])
                at = pl.ds(pl.multiple_of(((q % 4) * 2 + q // 4) * R, R), R)
                columns = pl.ds(pl.multiple_of(s * W, W), W)
                pih[at, columns] = high
                pil[at, columns] = low
                return carry

            lax.fori_loop(0, 8, piece, 0)

            @pl.when(s + 4 < SLABS)
            def _():
                slab_copy(s + 4, b).start()

            return carry

        lax.fori_loop(first, last, body, 0)

    def convert(j):
        def body(q, carry):
            high, low = split(gath[j, q])
            at = pl.ds(pl.multiple_of(q * R, R), R)
            bh[at, :] = high
            bl[at, :] = low
            return carry

        lax.fori_loop(0, 16, body, 0)

    def compute(j, pair):
        at = pl.ds(pl.multiple_of(pair * (2 * R), 2 * R), 2 * R)
        total = dot(pih[at, :], bh[...]) + dot(pih[at, :], bl[...]) + dot(pil[at, :], bh[...])
        part[j, pl.ds(pair * 2, 2)] = total.reshape(2, R, W)

    def rs(j, m):
        ss, rs_ = rs_s.at[j, m], rs_r.at[j, m]
        if m == 0:
            return remote(part.at[j, pl.ds(x2 * 2, 2)], x1r.at[j], ss, rs_, to_xf)
        if m == 1:
            return remote(part.at[j, pl.ds(xb * 2, 2)], x2b.at[j], ss, rs_, to_xb)
        if m == 2:
            return remote(part.at[j, pl.ds(xf * 2, 2)], x2f.at[j], ss, rs_, to_xf)
        return remote(part.at[j, x * 2 + (1 - zl)], zrec.at[j], ss, rs_, to_zp)

    def r1(j):
        rs(j, 0).wait_recv()
        at = pl.ds(xf * 2, 2)
        part[j, at] = part[j, at] + x1r[j]
        rs(j, 2).start()

    def r2(j):
        rs(j, 1).wait_recv()
        rs(j, 2).wait_recv()
        for q in (1 - zl, zl):
            part[j, x * 2 + q] = part[j, x * 2 + q] + x2f[j, q] + x2b[j, q]
        rs(j, 3).start()

    def sib_gram(j):
        return remote(gp.at[j, :, 1 - k], gsr.at[j], g_s.at[j], g_r.at[j], sib)

    def r3(j):
        rs(j, 3).wait_recv()
        product = part[j, x * 2 + zl] + zrec[j]
        out[:, j * H:(j + 1) * H] = -product[:, :H]
        out[:, 512 + j * H:512 + (j + 1) * H] = -product[:, H:]
        high, low = split(product)
        for i in range(8):
            at = pl.ds(i * H, H)
            tile = dot(pth[at, :], high) + dot(pth[at, :], low) + dot(ptl[at, :], high)
            gp[j, i] = tile.reshape(2, 64, W)
        sib_gram(j).start()

    def spread(j, i):
        z_, y_ = (z + i // 4) % 4, (y + i % 4) % 4
        source = gp.at[j, (z_ // 2) * 4 + y_, k, :, pl.ds(pl.multiple_of((z_ % 2) * H, H), H)]
        return remote(source, a2a.at[j, i], a_s.at[j, i], a_r.at[j, i], dev(z_, y_, x, k))

    def r4(j):
        sib_gram(j).wait_recv()
        for i in range(8):
            gp[j, i, k] = gp[j, i, k] + gsr[j, i]

        def body(i, carry):
            spread(j, i).start()
            return carry

        lax.fori_loop(1, 16, body, 0)

    def last(j):
        dx = (x - j + 4) % 4
        return remote(fsend.at[j], fin.at[dx], f_s.at[j], f_r.at[dx], dev(z, y, j, k))

    def r5(j):
        own = gp[j, zh * 4 + y, k, :, pl.ds(pl.multiple_of(zl * H, H), H)]

        def body(i, total):
            at = a2a.at[j, i]
            remote(at, at, a_s.at[j, i], a_r.at[j, i], sib).wait_recv()
            return total + a2a[j, i]

        total = lax.fori_loop(1, 16, body, own)
        fsend[j] = total

        @pl.when(x != j)
        def _():
            last(j).start()

    def r6(j):
        @pl.when(x == j)
        def _():
            total = saved[...] + fsend[j]
            for dx in range(1, 4):
                at = fin.at[dx]
                remote(at, at, f_s.at[j], f_r.at[dx], sib).wait_recv()
                total = total + fin[dx]
            diag[...] = total

    perm = remote(panel, rows, p_s, p_r, perm_to)
    perm_self = pltpu.make_async_copy(panel, rows, p_r)

    def perm_start():
        @pl.when(moves)
        def _():
            perm.start()

        @pl.when(jnp.logical_not(moves))
        def _():
            perm_self.start()

    def perm_take():
        @pl.when(moves)
        def _():
            perm.wait_recv()

        @pl.when(jnp.logical_not(moves))
        def _():
            perm_self.wait()

        for i in range(8):
            high, low = split(rows[:, i * H:(i + 1) * H].T)
            pth[i * H:(i + 1) * H, :] = high
            ptl[i * H:(i + 1) * H, :] = low

    p0(0)
    p0(1)
    split_slabs(0, 4)
    p1(0)
    split_slabs(4, 8)
    p2(0)
    p0(2)
    p1(1)
    split_slabs(8, 12)
    p3(0)
    p2(1)
    p4(0)
    perm_start()
    p5(0)

    services = {
        0: [lambda: (p0(3), p1(2)), lambda: p3(1), lambda: p2(2), lambda: (p4(1), p1(3), r1(0), p5(1))],
        1: [lambda: (p3(2), p2(3)), lambda: (p4(2), perm_take()), lambda: (p3(3), r2(0)), lambda: (p5(2), r1(1))],
        2: [lambda: (p4(3), r3(0)), lambda: r4(0), lambda: r2(1), lambda: (p5(3), r1(2))],
        3: [lambda: (r5(0), r3(1)), lambda: r4(1), lambda: r2(2), lambda: (r5(1), r1(3))],
    }
    for j in range(J):
        convert(j)
        compute(j, x2)
        rs(j, 0).start()
        services[j][0]()
        compute(j, xb)
        rs(j, 1).start()
        services[j][1]()
        compute(j, xf)
        services[j][2]()
        compute(j, x)
        services[j][3]()
    r3(2)
    r4(2)
    r2(3)
    r5(2)
    r3(3)
    r4(3)
    r5(3)
    for j in range(J):
        r6(j)

    for j in range(J):
        for m in range(16):
            ag(j, m).wait_send()
        for m in range(4):
            rs(j, m).wait_send()
        sib_gram(j).wait_send()

        def body(i, carry):
            spread(j, i).wait_send()
            return carry

        lax.fori_loop(1, 16, body, 0)

        @pl.when(x != j)
        def _():
            last(j).wait_send()

    @pl.when(moves)
    def _():
        perm.wait_send()


def shards(parent_inverse, panel, saved_diag):
    vmem = pl.BlockSpec(memory_space=pltpu.VMEM)
    hbm = pl.BlockSpec(memory_space=pl.ANY)
    dma = pltpu.SemaphoreType.DMA
    return pl.pallas_call(
        kernel,
        out_shape=(
            jax.ShapeDtypeStruct((R, 1024), F32),
            jax.ShapeDtypeStruct((64, H), F32),
        ),
        in_specs=[hbm, hbm, vmem],
        out_specs=(vmem, vmem),
        scratch_shapes=[
            pltpu.VMEM((8 * R, K), BF16),
            pltpu.VMEM((8 * R, K), BF16),
            pltpu.VMEM((J, 16, R, W), F32),
            pltpu.VMEM((K, W), BF16),
            pltpu.VMEM((K, W), BF16),
            pltpu.VMEM((J, R, W), F32),
            pltpu.VMEM((J, 2, R, W), F32),
            pltpu.VMEM((J, 2, R, W), F32),
            pltpu.VMEM((J, 2, R, W), F32),
            pltpu.VMEM((J, R, W), F32),
            pltpu.VMEM((J, 8, R, W), F32),
            pltpu.VMEM((R, 1024), F32),
            pltpu.VMEM((1024, R), BF16),
            pltpu.VMEM((1024, R), BF16),
            pltpu.VMEM((J, 8, 2, 64, W), F32),
            pltpu.VMEM((J, 8, 64, W), F32),
            pltpu.VMEM((J, 16, 64, H), F32),
            pltpu.VMEM((4, 64, H), F32),
            pltpu.VMEM((J, 64, H), F32),
            dma((4,)),
            dma((J, 2)),
            dma((J, 16)),
            dma((J, 16)),
            dma((J, 4)),
            dma((J, 4)),
            dma((J,)),
            dma((J,)),
            dma((J, 16)),
            dma((J, 16)),
            dma((J,)),
            dma((4,)),
            dma,
            dma,
        ],
        compiler_params=pltpu.CompilerParams(
            collective_id=0, has_side_effects=True, vmem_limit_bytes=67043328
        ),
    )(parent_inverse.reshape(8, R, K), panel, saved_diag)


def solution(mesh):
    in_specs = (P("row", "col"), P(("col", "row"), None), P("row", "col"))
    out_specs = (P(("row", "col"), None), P("row", "col"))
    return jax.shard_map(shards, mesh=mesh, in_specs=in_specs, out_specs=out_specs, check_vma=False)
```

```python
import jax
import jax.numpy as jnp
from jax import lax
from jax.experimental import pallas as pl
from jax.experimental.pallas import tpu as pltpu
from jax.sharding import PartitionSpec as P

MESH = pl.DeviceIdType.MESH
F32 = jnp.float32
BF16 = jnp.bfloat16
CHUNKS = ((0, (0,)), (1, (0, 1)), (2, (0, 1)), (3, (0, 1)), (0, (1,)))
J = len(CHUNKS)
WIDTHS = tuple(128 * len(zls) for _, zls in CHUNKS)
H = 128
R = 192
K = 3072
SLAB = 256
SLABS = K // SLAB
STAGES = tuple(j for j in range(J) if WIDTHS[j] == SLAB)[:3]

ORDER = (
    ("p0", 0), ("perm1",), ("p0", 1), ("sp", 4), ("sp", 5), ("sp", 6), ("sp", 7), ("sp", 8), ("sp", 9), ("sp", 10),
    ("sp", 11), ("p1a", 0), ("p1b", 0), ("p2", 0), ("p1a", 1), ("p1b", 1), ("p2", 1), ("p3", 0), ("p4b", 0),
    ("p4a", 0), ("p4c", 0), ("p0", 2), ("p4b", 1), ("p3", 1), ("p0", 3), ("cv", 0), ("A", 0), ("p4a", 1), ("p0", 4),
    ("BC", 0), ("p1a", 2), ("p1b", 2), ("D", 0), ("p4c", 1), ("p1b", 3), ("p2", 2), ("r1", 0), ("p1a", 3), ("p1b", 4),
    ("p1a", 4), ("cv", 1), ("A", 1), ("p3", 2), ("p2", 3), ("BC", 1), ("r2", 0), ("p4a", 2), ("p4b", 2), ("D", 1),
    ("p4c", 2), ("r1", 1), ("p4b", 3), ("p3", 4), ("p3", 3), ("p2", 4), ("cv", 2), ("r3", 0), ("perm2",), ("p4a", 3),
    ("A", 2), ("BC", 2), ("r2", 1), ("p4c", 3), ("p4a", 4), ("p4b", 4), ("p4c", 4), ("D", 2), ("r1", 2), ("cv", 3),
    ("A", 3), ("BC", 3), ("r2", 2), ("r3", 1), ("take",), ("gr", 0), ("gr", 1), ("r4", 0), ("r1", 3), ("D", 3),
    ("r3", 2), ("r4", 1), ("gr", 2), ("cv", 4), ("A", 4), ("r2", 3), ("r4", 2), ("BC", 4), ("r1", 4), ("D", 4),
    ("r3", 3), ("gr", 3), ("r5", 1), ("r2", 4), ("r5", 0), ("r4", 3), ("r3", 4), ("gr", 4), ("r5", 2), ("r4", 4),
    ("r5", 3), ("r5", 4), ("r6", 0), ("r6", 1), ("r6", 2), ("r6", 3), ("r6", 4),
)


def dot(a, b):
    return jnp.dot(a, b, preferred_element_type=F32)


def split(value):
    high = value.astype(BF16)
    return high, (value - high.astype(F32)).astype(BF16)


def kernel(*refs):
    pi, panel, out, diag, pih, pil, bh, bl, rows, mid, pth, ptl, fin = refs[:13]
    rest = refs[13:]
    gath, x1r, x2f, x2b, zrec, part, gp, gsr, a2a, fsend = (rest[i * J:(i + 1) * J] for i in range(10))
    (pisem, locsem, ag_s, ag_r, rs_s, rs_r, g_s, g_r, a_s, a_r, f_s, f_r,
     p1_s, p1_r, p2_s, p2_r) = rest[10 * J:]
    r, c = lax.axis_index("row"), lax.axis_index("col")
    zh, y, k = r // 8, (r // 2) % 4, r % 2
    zl, x = c // 4, c % 4
    z = zh * 2 + zl
    d = 1 - 2 * k

    def dev(z_, y_, x_, k_):
        return ((z_ // 2) * 8 + y_ * 2 + k_, (z_ % 2) * 4 + x_)

    def slot(zh_, y_, k_):
        return zh_ * 8 + y_ * 2 + k_

    yf, yb, y2 = (y + d + 4) % 4, (y - d + 4) % 4, (y + 2) % 4
    xf, xb, x2 = (x + d + 4) % 4, (x - d + 4) % 4, (x + 2) % 4
    zp, zt = zh * 2 + (1 - zl), (z + 2) % 4
    zo = 1 - zh
    sib = dev(z, y, x, 1 - k)
    to_yf, to_yb = dev(z, yf, x, k), dev(z, yb, x, k)
    to_zt, to_zp = dev(zt, y, x, k), dev(zp, y, x, k)
    to_xf, to_xb = dev(z, y, xf, k), dev(z, y, xb, k)

    def remote(src, dst, ss, rs, to):
        return pltpu.make_async_remote_copy(
            src_ref=src, dst_ref=dst, send_sem=ss, recv_sem=rs, device_id=to, device_id_type=MESH
        )

    def arrived(at, ss, rs):
        remote(at, at, ss, rs, sib).wait_recv()

    def sent(at, ss):
        remote(at, at, ss, p1_s, sib).wait_send()

    def columns(j, h):
        x_, zls = CHUNKS[j]
        return pl.ds((zls[h] * 4 + x_) * H, H)

    def own_copy(j, h):
        return pltpu.make_async_copy(
            panel.at[:, columns(j, h)], gath[j].at[r, :, pl.ds(h * H, H)], locsem.at[j, h]
        )

    def slab_copy(s):
        b = s % 3
        return pltpu.make_async_copy(pi.at[:, :, pl.ds(s * SLAB, SLAB)], part[STAGES[b]], pisem.at[b])

    for h in range(len(CHUNKS[0][1])):
        own_copy(0, h).start()
    for s in range(3):
        slab_copy(s).start()
    for j in range(1, J):
        for h in range(len(CHUNKS[j][1])):
            own_copy(j, h).start()

    barrier = pltpu.get_barrier_semaphore()
    peers = [to_yf, to_yb, to_zt, to_zp, sib]
    for dx in range(1, 4):
        for k_ in range(2):
            peers.append(dev(z, y, (x + dx) % 4, k_))
    for to in peers:
        pl.semaphore_signal(barrier, inc=1, device_id=to, device_id_type=MESH)

    def split_slab(s):
        b = part[STAGES[s % 3]]
        slab_copy(s).wait()

        def piece(q, carry):
            high, low = split(b[q])
            at = pl.ds(pl.multiple_of(((q % 4) * 2 + q // 4) * R, R), R)
            pih[at, s * SLAB:(s + 1) * SLAB] = high
            pil[at, s * SLAB:(s + 1) * SLAB] = low
            return carry

        lax.fori_loop(0, 8, piece, 0)
        if s + 3 < SLABS:
            slab_copy(s + 3).start()

    got = [slot(zh, yb, k), slot(zh, yf, k), slot(zo, y, k), None, slot(zo, yb, k), slot(zo, yf, k),
           slot(zh, y2, k), slot(zo, y2, k)]
    sib_slots = [slot(zh, y, k), got[0], got[1], got[2], got[6], got[4], got[5], got[7]]
    def ag(j, m):
        if m >= 8:
            source, to = sib_slots[m - 8], sib
        else:
            source = {0: r, 1: r, 2: r, 4: got[2], 5: got[2], 6: got[0], 7: got[6]}[m]
            to = {1: to_yb, 5: to_yb, 2: to_zt, 7: to_zt}.get(m, to_yf)
        at = gath[j].at[source]
        return remote(at, at, ag_s.at[j], ag_r.at[j, min(m, 8)], to)

    def ag_wait(j, m):
        at = gath[j].at[got[m]]
        arrived(at, ag_s.at[j], ag_r.at[j, m])

    def p0(j):
        for h in range(len(CHUNKS[j][1])):
            own_copy(j, h).wait()
        for m in (0, 2, 1, 8):
            ag(j, m).start()

    def relay(wait, *starts):
        def step(j):
            ag_wait(j, wait)
            for m in starts:
                ag(j, m).start()
        return step

    def cv(j):
        arrived(gath[j].at[0:8], ag_s.at[j], ag_r.at[j, 8])

        def body(q, carry):
            high, low = split(gath[j][q])
            at = pl.ds(pl.multiple_of(q * R, R), R)
            bh[at, :WIDTHS[j]] = high
            bl[at, :WIDTHS[j]] = low
            return carry

        lax.fori_loop(0, 16, body, 0)

    def compute(j, pair):
        at = pl.ds(pl.multiple_of(pair * (2 * R), 2 * R), 2 * R)
        high, low = bh[:, :WIDTHS[j]], bl[:, :WIDTHS[j]]
        total = dot(pih[at, :], high) + dot(pih[at, :], low) + dot(pil[at, :], high)
        part[j][pl.ds(pair * 2, 2)] = total.reshape(2, R, WIDTHS[j])

    def rs(j, m):
        ss, rs_ = rs_s.at[j], rs_r.at[j, m]
        if m == 0:
            return remote(part[j].at[pl.ds(x2 * 2, 2)], x1r[j], ss, rs_, to_xf)
        if m == 1:
            return remote(part[j].at[pl.ds(xb * 2, 2)], x2b[j], ss, rs_, to_xb)
        if m == 2:
            return remote(part[j].at[pl.ds(xf * 2, 2)], x2f[j], ss, rs_, to_xf)
        return remote(part[j].at[x * 2 + (1 - zl)], zrec[j], ss, rs_, to_zp)

    def qa(j):
        compute(j, x2)
        rs(j, 0).start()

    def qbc(j):
        def body(i, carry):
            compute(j, jnp.where(i == 0, xb, xf))

            @pl.when(i == 0)
            def _():
                rs(j, 1).start()

            return carry

        lax.fori_loop(0, 2, body, 0)

    def qd(j):
        compute(j, x)

    def r1(j):
        rs(j, 0).wait_recv()
        at = pl.ds(xf * 2, 2)
        part[j][at] = part[j][at] + x1r[j][...]
        rs(j, 2).start()

    def r2(j):
        rs(j, 1).wait_recv()
        rs(j, 2).wait_recv()
        q = 1 - zl
        part[j][x * 2 + q] = part[j][x * 2 + q] + x2f[j][q] + x2b[j][q]
        rs(j, 3).start()
        part[j][x * 2 + zl] = part[j][x * 2 + zl] + x2f[j][zl] + x2b[j][zl]

    def r3(j):
        rs(j, 3).wait_recv()
        product = part[j][x * 2 + zl] + zrec[j][...]
        part[j][x * 2 + zl] = product
        for h in range(len(CHUNKS[j][1])):
            out[:, columns(j, h)] = product[:, h * H:(h + 1) * H]

    def sib_gram(j):
        return remote(gp[j].at[:, 1 - k], gsr[j], g_s.at[j], g_r.at[j], sib)

    def gr(j):
        high, low = split(part[j][x * 2 + zl])
        for i in range(8):
            at = pl.ds(i * H, H)
            tile = dot(pth[at, :], high) + dot(pth[at, :], low) + dot(ptl[at, :], high)
            gp[j][i] = tile.reshape(2, 64, WIDTHS[j])
        sib_gram(j).start()

    def gram_to(j, i):
        zls = CHUNKS[j][1]
        if len(zls) == 2:
            z_ = (z + i // 4) % 4
            at = z_ % 2
        else:
            z_ = ((zh + i // 4) % 2) * 2 + zls[0]
            at = 0
        y_ = (y + i % 4) % 4
        source = gp[j].at[(z_ // 2) * 4 + y_, k, :, pl.ds(pl.multiple_of(at * H, H), H)]
        s = ((z_ - z + 4) % 4) * 4 + i % 4
        return remote(source, a2a[j].at[s], a_s.at[j], a_r.at[j], dev(z_, y_, x, k))

    def r4(j):
        arrived(gsr[j], g_s.at[j], g_r.at[j])
        for i in range(8):
            gp[j][i, k] = gp[j][i, k] + gsr[j][i]
        both = len(CHUNKS[j][1]) == 2
        for i in range(8 * len(CHUNKS[j][1])):
            if i or not both:
                copy = gram_to(j, i)
                copy.start() if i else pl.when(zl != CHUNKS[j][1][0])(copy.start)

    def takes(j, act):
        zls = CHUNKS[j][1]
        if len(zls) == 2:
            act()
        else:
            pl.when(zl == zls[0])(act)

    def last(j):
        x_ = CHUNKS[j][0]
        dx = (x - x_ + 4) % 4
        return remote(fsend[j], fin.at[dx], f_s.at[j], f_r.at[dx], dev(z, y, x_, k))

    def r5(j):
        def act():
            at = zl * H if len(CHUNKS[j][1]) == 2 else 0
            own = gp[j][zh * 4 + y, k, :, pl.ds(pl.multiple_of(at, H), H)]

            arrived(a2a[j].at[1:16], a_s.at[j], a_r.at[j])
            parts = [own] + [a2a[j][i] for i in range(1, 16)]
            while len(parts) > 1:
                parts = [a + b for a, b in zip(parts[::2], parts[1::2])]
            fsend[j][...] = parts[0]

            @pl.when(x != CHUNKS[j][0])
            def _():
                last(j).start()

        takes(j, act)

    def r6(j):
        def act():
            @pl.when(x == CHUNKS[j][0])
            def _():
                total = fsend[j][...]
                for dx in range(1, 4):
                    arrived(fin.at[dx], f_s.at[j], f_r.at[dx])
                    total = total + fin[dx]
                diag[...] = total

        takes(j, act)

    to_mid = dev(z, y, 2 * (y % 2) + k, x % 2)
    stays = jnp.logical_and(x == 2 * (y % 2) + k, x % 2 == k)
    is_mid = x // 2 == y % 2
    lands = jnp.logical_and(
        jnp.logical_and(y % 2 == k, zl == zh),
        jnp.logical_and(jnp.logical_and(y // 2 == zl, zh == k), is_mid),
    )
    perm1_copy = remote(panel, mid.at[x // 2], p1_s, p1_r.at[x // 2], to_mid)
    perm1_self = pltpu.make_async_copy(panel, mid.at[x // 2], p1_r.at[x // 2])

    def perm1():
        @pl.when(stays)
        def _():
            perm1_self.start()

        @pl.when(jnp.logical_not(stays))
        def _():
            perm1_copy.start()

    def perm2_copy(m):
        return remote(mid.at[m], rows, p2_s.at[m], p2_r, dev(2 * zl + y // 2, 2 * m + k, x, zh))

    def perm2_self(m):
        return pltpu.make_async_copy(mid.at[m], rows, p2_r)

    def perm2():
        @pl.when(is_mid)
        def _():
            for m in range(2):
                here = jnp.logical_and(stays, x // 2 == m)

                @pl.when(here)
                def _():
                    pltpu.make_async_copy(panel, mid.at[m], p1_r.at[m]).wait()

                @pl.when(jnp.logical_not(here))
                def _():
                    arrived(mid.at[m], p1_s, p1_r.at[m])

            for m in range(2):
                here = jnp.logical_and(lands, y // 2 == m)

                @pl.when(here)
                def _():
                    perm2_self(m).start()

                @pl.when(jnp.logical_not(here))
                def _():
                    perm2_copy(m).start()

    def take():
        @pl.when(lands)
        def _():
            perm2_self(0).wait()

        @pl.when(jnp.logical_not(lands))
        def _():
            arrived(rows, p2_s.at[0], p2_r)

        for i in range(8):
            high, low = split(rows[:, i * H:(i + 1) * H].T)
            pth[i * H:(i + 1) * H, :] = high
            ptl[i * H:(i + 1) * H, :] = low

    for s in range(4):
        split_slab(s)
    pl.semaphore_wait(barrier, len(peers))

    steps = {
        "sp": split_slab, "p0": p0, "p1a": relay(0, 6, 9), "p1b": relay(1, 10), "p2": relay(2, 4, 5, 11),
        "p3": relay(6, 7, 12), "p4a": relay(4, 13), "p4b": relay(5, 14), "p4c": relay(7, 15),
        "cv": cv, "A": qa, "BC": qbc, "D": qd, "r1": r1, "r2": r2, "r3": r3, "gr": gr,
        "r4": r4, "r5": r5, "r6": r6, "perm1": perm1, "perm2": perm2, "take": take,
    }
    for step in ORDER:
        steps[step[0]](*step[1:])

    for j in range(J):
        sent(gath[j].at[0:15], ag_s.at[j])
        sent(gath[j].at[0:7], rs_s.at[j])
        sib_gram(j).wait_send()
        if len(CHUNKS[j][1]) == 2:
            sent(a2a[j].at[0:15], a_s.at[j])
        else:
            @pl.when(zl == CHUNKS[j][1][0])
            def _():
                sent(a2a[j].at[0:7], a_s.at[j])

            @pl.when(zl != CHUNKS[j][1][0])
            def _():
                sent(a2a[j].at[0:8], a_s.at[j])

        def final(j=j):
            @pl.when(x != CHUNKS[j][0])
            def _():
                last(j).wait_send()

        takes(j, final)

    @pl.when(jnp.logical_not(stays))
    def _():
        perm1_copy.wait_send()

    @pl.when(is_mid)
    def _():
        for m in range(2):
            @pl.when(jnp.logical_not(jnp.logical_and(lands, y // 2 == m)))
            def _():
                perm2_copy(m).wait_send()


def shards(parent_inverse, panel, saved_diag):
    vmem = pl.BlockSpec(memory_space=pltpu.VMEM)
    hbm = pl.BlockSpec(memory_space=pl.ANY)
    dma = pltpu.SemaphoreType.DMA

    def each(*shape):
        return [pltpu.VMEM(shape + (w,), F32) for w in WIDTHS]

    product, gram = pl.pallas_call(
        kernel,
        out_shape=(
            jax.ShapeDtypeStruct((R, 1024), F32),
            jax.ShapeDtypeStruct((64, H), F32),
        ),
        in_specs=[hbm, hbm],
        out_specs=(vmem, vmem),
        scratch_shapes=[
            pltpu.VMEM((8 * R, K), BF16),
            pltpu.VMEM((8 * R, K), BF16),
            pltpu.VMEM((K, max(WIDTHS)), BF16),
            pltpu.VMEM((K, max(WIDTHS)), BF16),
            pltpu.VMEM((R, 1024), F32),
            pltpu.VMEM((2, R, 1024), F32),
            pltpu.VMEM((1024, R), BF16),
            pltpu.VMEM((1024, R), BF16),
            pltpu.VMEM((4, 64, H), F32),
            *each(16, R),
            *each(2, R),
            *each(2, R),
            *each(2, R),
            *each(R),
            *each(8, R),
            *each(8, 2, 64),
            *each(8, 64),
            *[pltpu.VMEM((16, 64, H), F32) for _ in range(J)],
            *[pltpu.VMEM((64, H), F32) for _ in range(J)],
            dma((3,)),
            dma((J, 2)),
            dma((J,)),
            dma((J, 9)),
            dma((J,)),
            dma((J, 4)),
            dma((J,)),
            dma((J,)),
            dma((J,)),
            dma((J,)),
            dma((J,)),
            dma((4,)),
            dma,
            dma((2,)),
            dma((2,)),
            dma,
        ],
        compiler_params=pltpu.CompilerParams(
            collective_id=0, has_side_effects=True, vmem_limit_bytes=67043328
        ),
    )(parent_inverse.reshape(8, R, K), panel)
    return -product, saved_diag + gram


def solution(mesh):
    in_specs = (P("row", "col"), P(("col", "row"), None), P("row", "col"))
    out_specs = (P(("row", "col"), None), P("row", "col"))
    return jax.shard_map(shards, mesh=mesh, in_specs=in_specs, out_specs=out_specs, check_vma=False)
```

```python
import jax
import jax.numpy as jnp
from jax import lax
from jax.experimental import pallas as pl
from jax.experimental.pallas import tpu as pltpu
from jax.sharding import PartitionSpec as P

MESH = pl.DeviceIdType.MESH
F32 = jnp.float32
BF16 = jnp.bfloat16
CHUNKS = ((0, (0,)), (1, (0, 1)), (2, (0, 1)), (3, (0, 1)), (0, (1,)))
J = len(CHUNKS)
WIDTHS = tuple(128 * len(zls) for _, zls in CHUNKS)
H = 128
R = 192
K = 3072
SLAB = 256
SLABS = K // SLAB
STAGES = tuple(j for j in range(J) if WIDTHS[j] == SLAB)[:3]

ACROSS = ()

ORDER = (
    ("p0", 0), ("perm1",), ("p0", 1), ("sp", 4), ("sp", 5), ("sp", 6), ("sp", 7), ("sp", 8), ("sp", 9), ("sp", 10),
    ("sp", 11), ("p1a", 0), ("p1b", 0), ("p2", 0), ("p1a", 1), ("p1b", 1), ("p2", 1), ("p3", 0), ("p4b", 0),
    ("p4a", 0), ("p4c", 0), ("p0", 2), ("p4b", 1), ("p3", 1), ("p0", 3), ("cv", 0), ("A", 0), ("p4a", 1), ("p0", 4),
    ("BC", 0), ("p1a", 2), ("p1b", 2), ("D", 0), ("p4c", 1), ("p1b", 3), ("p2", 2), ("r1", 0), ("p1a", 3), ("p1b", 4),
    ("p1a", 4), ("cv", 1), ("A", 1), ("p3", 2), ("p2", 3), ("BC", 1), ("r2", 0), ("p4a", 2), ("p4b", 2), ("D", 1),
    ("p4c", 2), ("r1", 1), ("p4b", 3), ("p3", 4), ("p3", 3), ("p2", 4), ("cv", 2), ("r3", 0), ("perm2",), ("p4a", 3),
    ("A", 2), ("BC", 2), ("r2", 1), ("p4c", 3), ("p4a", 4), ("p4b", 4), ("p4c", 4), ("D", 2), ("r1", 2), ("cv", 3),
    ("A", 3), ("BC", 3), ("r2", 2), ("r3", 1), ("take",), ("gr", 0), ("gr", 1), ("r4", 0), ("r1", 3), ("D", 3),
    ("r3", 2), ("r4", 1), ("gr", 2), ("cv", 4), ("A", 4), ("r2", 3), ("r4", 2), ("BC", 4), ("r1", 4), ("D", 4),
    ("r3", 3), ("gr", 3), ("r5", 1), ("r2", 4), ("r5", 0), ("r4", 3), ("r3", 4), ("gr", 4), ("r5", 2), ("r4", 4),
    ("r5", 3), ("r5", 4), ("r6", 0), ("r6", 1), ("r6", 2), ("r6", 3), ("r6", 4),
)


def dot(a, b):
    return jnp.dot(a, b, preferred_element_type=F32)


def split(value):
    high = value.astype(BF16)
    return high, (value - high.astype(F32)).astype(BF16)


def kernel(*refs):
    pi, panel, out, diag, pih, pil, bh, bl, rows, mid, pth, ptl, fin = refs[:13]
    rest = refs[13:]
    gath, x1r, x2f, x2b, zrec, part, gp, gsr, a2a, fsend = (rest[i * J:(i + 1) * J] for i in range(10))
    (pisem, locsem, ag_s, ag_r, rs_s, rs_r, g_s, g_r, a_s, a_r, f_s, f_r,
     p1_s, p1_r, p2_s, p2_r) = rest[10 * J:]
    r, c = lax.axis_index("row"), lax.axis_index("col")
    zh, y, k = r // 8, (r // 2) % 4, r % 2
    zl, x = c // 4, c % 4
    z = zh * 2 + zl
    d = 1 - 2 * k

    def dev(z_, y_, x_, k_):
        return ((z_ // 2) * 8 + y_ * 2 + k_, (z_ % 2) * 4 + x_)

    def slot(zh_, y_, k_):
        return zh_ * 8 + y_ * 2 + k_

    yf, yb, y2 = (y + d + 4) % 4, (y - d + 4) % 4, (y + 2) % 4
    xf, xb, x2 = (x + d + 4) % 4, (x - d + 4) % 4, (x + 2) % 4
    zp, zt = zh * 2 + (1 - zl), (z + 2) % 4
    zo = 1 - zh
    sib = dev(z, y, x, 1 - k)
    to_yf, to_yb = dev(z, yf, x, k), dev(z, yb, x, k)
    to_zt, to_zp = dev(zt, y, x, k), dev(zp, y, x, k)
    to_xf, to_xb = dev(z, y, xf, k), dev(z, y, xb, k)

    def remote(src, dst, ss, rs, to):
        return pltpu.make_async_remote_copy(
            src_ref=src, dst_ref=dst, send_sem=ss, recv_sem=rs, device_id=to, device_id_type=MESH
        )

    def arrived(at, ss, rs):
        remote(at, at, ss, rs, sib).wait_recv()

    def sent(at, ss):
        remote(at, at, ss, p1_s, sib).wait_send()

    def columns(j, h):
        x_, zls = CHUNKS[j]
        return pl.ds((zls[h] * 4 + x_) * H, H)

    def own_copy(j, h):
        return pltpu.make_async_copy(
            panel.at[:, columns(j, h)], gath[j].at[r, :, pl.ds(h * H, H)], locsem.at[j, h]
        )

    def slab_copy(s):
        b = s % 3
        return pltpu.make_async_copy(pi.at[:, :, pl.ds(s * SLAB, SLAB)], part[STAGES[b]], pisem.at[b])

    for h in range(len(CHUNKS[0][1])):
        own_copy(0, h).start()
    for s in range(3):
        slab_copy(s).start()
    for j in range(1, J):
        for h in range(len(CHUNKS[j][1])):
            own_copy(j, h).start()

    barrier = pltpu.get_barrier_semaphore()
    peers = [to_yf, to_yb, to_zt, to_zp, sib]
    for dx in range(1, 4):
        for k_ in range(2):
            peers.append(dev(z, y, (x + dx) % 4, k_))
    for to in peers:
        pl.semaphore_signal(barrier, inc=1, device_id=to, device_id_type=MESH)

    def split_slab(s):
        b = part[STAGES[s % 3]]
        slab_copy(s).wait()

        def piece(q, carry):
            high, low = split(b[q])
            at = pl.ds(pl.multiple_of(((q % 4) * 2 + q // 4) * R, R), R)
            pih[at, s * SLAB:(s + 1) * SLAB] = high
            pil[at, s * SLAB:(s + 1) * SLAB] = low
            return carry

        lax.fori_loop(0, 8, piece, 0)
        if s + 3 < SLABS:
            slab_copy(s + 3).start()

    got = [slot(zh, yb, k), slot(zh, yf, k), slot(zo, y, k), None, slot(zo, yb, k), slot(zo, yf, k),
           slot(zh, y2, k), slot(zo, y2, k)]
    sib_slots = [slot(zh, y, k), got[0], got[1], got[2], got[6], got[4], got[5], got[7]]
    def ag(j, m):
        if m >= 8:
            source, to = sib_slots[m - 8], sib
        else:
            source = {0: r, 1: r, 2: r, 4: got[2], 5: got[2], 6: got[0], 7: got[6]}[m]
            to = {1: to_yb, 5: to_yb, 2: to_zt, 7: to_zt}.get(m, to_yf)
        at = gath[j].at[source]
        return remote(at, at, ag_s.at[j], ag_r.at[j, min(m, 8)], to)

    def ag_wait(j, m):
        at = gath[j].at[got[m]]
        arrived(at, ag_s.at[j], ag_r.at[j, m])

    def p0(j):
        for h in range(len(CHUNKS[j][1])):
            own_copy(j, h).wait()
        for m in (0, 2, 1, 8):
            ag(j, m).start()

    def relay(wait, *starts):
        def step(j):
            ag_wait(j, wait)
            for m in starts:
                ag(j, m).start()
        return step

    def cv(j):
        arrived(gath[j].at[0:8], ag_s.at[j], ag_r.at[j, 8])

        def body(q, carry):
            high, low = split(gath[j][q])
            at = pl.ds(pl.multiple_of(q * R, R), R)
            if WIDTHS[j] == H:
                bh[at, :H] = high
                bh[at, H:] = low
            else:
                bh[at, :] = high
                bl[at, :] = low
            return carry

        lax.fori_loop(0, 16, body, 0)

    def compute(j, pair):
        at = pl.ds(pl.multiple_of(pair * (2 * R), 2 * R), 2 * R)
        if WIDTHS[j] == H:
            wide = dot(pih[at, :], bh[...])
            total = wide[:, :H] + wide[:, H:] + dot(pil[at, :], bh[:, :H])
        else:
            total = dot(pih[at, :], bh[...]) + dot(pih[at, :], bl[...]) + dot(pil[at, :], bh[...])
        part[j][pl.ds(pair * 2, 2)] = total.reshape(2, R, WIDTHS[j])

    def rs(j, m):
        ss, rs_ = rs_s.at[j], rs_r.at[j, m]
        if m == 0 and j in ACROSS:
            return remote(part[j].at[x2 * 2 + zl], x1r[j].at[0], ss, rs_, to_xf)
        if m == 0:
            return remote(part[j].at[pl.ds(x2 * 2, 2)], x1r[j], ss, rs_, to_xf)
        if m == 4:
            return remote(part[j].at[x2 * 2 + (1 - zl)], x1r[j].at[1], ss, rs_, to_zp)
        if m == 1:
            return remote(part[j].at[pl.ds(xb * 2, 2)], x2b[j], ss, rs_, to_xb)
        if m == 2:
            return remote(part[j].at[pl.ds(xf * 2, 2)], x2f[j], ss, rs_, to_xf)
        return remote(part[j].at[x * 2 + (1 - zl)], zrec[j], ss, rs_, to_zp)

    def qa(j):
        compute(j, x2)
        rs(j, 4 if j in ACROSS else 0).start()

    def r0(j):
        rs(j, 4).wait_recv()
        part[j][x2 * 2 + zl] = part[j][x2 * 2 + zl] + x1r[j][1]
        rs(j, 0).start()

    def qbc(j):
        def body(i, carry):
            compute(j, jnp.where(i == 0, xb, xf))

            @pl.when(i == 0)
            def _():
                rs(j, 1).start()

            return carry

        lax.fori_loop(0, 2, body, 0)

    def qd(j):
        compute(j, x)

    def r1(j):
        rs(j, 0).wait_recv()
        if j in ACROSS:
            part[j][xf * 2 + zl] = part[j][xf * 2 + zl] + x1r[j][0]
        else:
            at = pl.ds(xf * 2, 2)
            part[j][at] = part[j][at] + x1r[j][...]
        rs(j, 2).start()

    def r2(j):
        rs(j, 1).wait_recv()
        rs(j, 2).wait_recv()
        q = 1 - zl
        part[j][x * 2 + q] = part[j][x * 2 + q] + x2f[j][q] + x2b[j][q]
        rs(j, 3).start()
        part[j][x * 2 + zl] = part[j][x * 2 + zl] + x2f[j][zl] + x2b[j][zl]

    def r3(j):
        rs(j, 3).wait_recv()
        product = part[j][x * 2 + zl] + zrec[j][...]
        part[j][x * 2 + zl] = product
        for h in range(len(CHUNKS[j][1])):
            out[:, columns(j, h)] = product[:, h * H:(h + 1) * H]

    def sib_gram(j):
        return remote(gp[j].at[:, 1 - k], gsr[j], g_s.at[j], g_r.at[j], sib)

    def gr(j):
        high, low = split(part[j][x * 2 + zl])
        for i in range(8):
            at = pl.ds(i * H, H)
            tile = dot(pth[at, :], high) + dot(pth[at, :], low) + dot(ptl[at, :], high)
            gp[j][i] = tile.reshape(2, 64, WIDTHS[j])
        sib_gram(j).start()

    def gram_to(j, i):
        zls = CHUNKS[j][1]
        if len(zls) == 2:
            z_ = (z + i // 4) % 4
            at = z_ % 2
        else:
            z_ = ((zh + i // 4) % 2) * 2 + zls[0]
            at = 0
        y_ = (y + i % 4) % 4
        source = gp[j].at[(z_ // 2) * 4 + y_, k, :, pl.ds(pl.multiple_of(at * H, H), H)]
        s = ((z_ - z + 4) % 4) * 4 + i % 4
        return remote(source, a2a[j].at[s], a_s.at[j], a_r.at[j], dev(z_, y_, x, k))

    def r4(j):
        arrived(gsr[j], g_s.at[j], g_r.at[j])
        for i in range(8):
            gp[j][i, k] = gp[j][i, k] + gsr[j][i]
        both = len(CHUNKS[j][1]) == 2
        for i in range(8 * len(CHUNKS[j][1])):
            if i or not both:
                copy = gram_to(j, i)
                copy.start() if i else pl.when(zl != CHUNKS[j][1][0])(copy.start)

    def takes(j, act):
        zls = CHUNKS[j][1]
        if len(zls) == 2:
            act()
        else:
            pl.when(zl == zls[0])(act)

    def last(j):
        x_ = CHUNKS[j][0]
        dx = (x - x_ + 4) % 4
        return remote(fsend[j], fin.at[dx], f_s.at[j], f_r.at[dx], dev(z, y, x_, k))

    def r5(j):
        def act():
            at = zl * H if len(CHUNKS[j][1]) == 2 else 0
            own = gp[j][zh * 4 + y, k, :, pl.ds(pl.multiple_of(at, H), H)]

            arrived(a2a[j].at[1:16], a_s.at[j], a_r.at[j])
            parts = [own] + [a2a[j][i] for i in range(1, 16)]
            while len(parts) > 1:
                parts = [a + b for a, b in zip(parts[::2], parts[1::2])]
            fsend[j][...] = parts[0]

            @pl.when(x != CHUNKS[j][0])
            def _():
                last(j).start()

        takes(j, act)

    def r6(j):
        def act():
            @pl.when(x == CHUNKS[j][0])
            def _():
                total = fsend[j][...]
                for dx in range(1, 4):
                    arrived(fin.at[dx], f_s.at[j], f_r.at[dx])
                    total = total + fin[dx]
                diag[...] = total

        takes(j, act)

    to_mid = dev(z, y, 2 * (y % 2) + k, x % 2)
    stays = jnp.logical_and(x == 2 * (y % 2) + k, x % 2 == k)
    is_mid = x // 2 == y % 2
    lands = jnp.logical_and(
        jnp.logical_and(y % 2 == k, zl == zh),
        jnp.logical_and(jnp.logical_and(y // 2 == zl, zh == k), is_mid),
    )
    perm1_copy = remote(panel, mid.at[x // 2], p1_s, p1_r.at[x // 2], to_mid)
    perm1_self = pltpu.make_async_copy(panel, mid.at[x // 2], p1_r.at[x // 2])

    def perm1():
        @pl.when(stays)
        def _():
            perm1_self.start()

        @pl.when(jnp.logical_not(stays))
        def _():
            perm1_copy.start()

    def perm2_copy(m):
        return remote(mid.at[m], rows, p2_s.at[m], p2_r, dev(2 * zl + y // 2, 2 * m + k, x, zh))

    def perm2_self(m):
        return pltpu.make_async_copy(mid.at[m], rows, p2_r)

    def perm2():
        @pl.when(is_mid)
        def _():
            for m in range(2):
                here = jnp.logical_and(stays, x // 2 == m)

                @pl.when(here)
                def _():
                    pltpu.make_async_copy(panel, mid.at[m], p1_r.at[m]).wait()

                @pl.when(jnp.logical_not(here))
                def _():
                    arrived(mid.at[m], p1_s, p1_r.at[m])

            for m in range(2):
                here = jnp.logical_and(lands, y // 2 == m)

                @pl.when(here)
                def _():
                    perm2_self(m).start()

                @pl.when(jnp.logical_not(here))
                def _():
                    perm2_copy(m).start()

    def take():
        @pl.when(lands)
        def _():
            perm2_self(0).wait()

        @pl.when(jnp.logical_not(lands))
        def _():
            arrived(rows, p2_s.at[0], p2_r)

        for i in range(8):
            high, low = split(rows[:, i * H:(i + 1) * H].T)
            pth[i * H:(i + 1) * H, :] = high
            ptl[i * H:(i + 1) * H, :] = low

    for s in range(4):
        split_slab(s)
    pl.semaphore_wait(barrier, len(peers))

    steps = {
        "sp": split_slab, "p0": p0, "p1a": relay(0, 6, 9), "p1b": relay(1, 10), "p2": relay(2, 4, 5, 11),
        "p3": relay(6, 7, 12), "p4a": relay(4, 13), "p4b": relay(5, 14), "p4c": relay(7, 15),
        "cv": cv, "A": qa, "BC": qbc, "D": qd, "r0": r0, "r1": r1, "r2": r2, "r3": r3, "gr": gr,
        "r4": r4, "r5": r5, "r6": r6, "perm1": perm1, "perm2": perm2, "take": take,
    }
    for step in ORDER:
        steps[step[0]](*step[1:])

    for j in range(J):
        sent(gath[j].at[0:15], ag_s.at[j])
        sent(gath[j].at[0:7], rs_s.at[j])
        sib_gram(j).wait_send()
        if len(CHUNKS[j][1]) == 2:
            sent(a2a[j].at[0:15], a_s.at[j])
        else:
            @pl.when(zl == CHUNKS[j][1][0])
            def _():
                sent(a2a[j].at[0:7], a_s.at[j])

            @pl.when(zl != CHUNKS[j][1][0])
            def _():
                sent(a2a[j].at[0:8], a_s.at[j])

        def final(j=j):
            @pl.when(x != CHUNKS[j][0])
            def _():
                last(j).wait_send()

        takes(j, final)

    @pl.when(jnp.logical_not(stays))
    def _():
        perm1_copy.wait_send()

    @pl.when(is_mid)
    def _():
        for m in range(2):
            @pl.when(jnp.logical_not(jnp.logical_and(lands, y // 2 == m)))
            def _():
                perm2_copy(m).wait_send()


def shards(parent_inverse, panel, saved_diag):
    vmem = pl.BlockSpec(memory_space=pltpu.VMEM)
    hbm = pl.BlockSpec(memory_space=pl.ANY)
    dma = pltpu.SemaphoreType.DMA

    def each(*shape):
        return [pltpu.VMEM(shape + (w,), F32) for w in WIDTHS]

    product, gram = pl.pallas_call(
        kernel,
        out_shape=(
            jax.ShapeDtypeStruct((R, 1024), F32),
            jax.ShapeDtypeStruct((64, H), F32),
        ),
        in_specs=[hbm, hbm],
        out_specs=(vmem, vmem),
        scratch_shapes=[
            pltpu.VMEM((8 * R, K), BF16),
            pltpu.VMEM((8 * R, K), BF16),
            pltpu.VMEM((K, max(WIDTHS)), BF16),
            pltpu.VMEM((K, max(WIDTHS)), BF16),
            pltpu.VMEM((R, 1024), F32),
            pltpu.VMEM((2, R, 1024), F32),
            pltpu.VMEM((1024, R), BF16),
            pltpu.VMEM((1024, R), BF16),
            pltpu.VMEM((4, 64, H), F32),
            *each(16, R),
            *each(2, R),
            *each(2, R),
            *each(2, R),
            *each(R),
            *each(8, R),
            *each(8, 2, 64),
            *each(8, 64),
            *[pltpu.VMEM((16, 64, H), F32) for _ in range(J)],
            *[pltpu.VMEM((64, H), F32) for _ in range(J)],
            dma((3,)),
            dma((J, 2)),
            dma((J,)),
            dma((J, 9)),
            dma((J,)),
            dma((J, 5)),
            dma((J,)),
            dma((J,)),
            dma((J,)),
            dma((J,)),
            dma((J,)),
            dma((4,)),
            dma,
            dma((2,)),
            dma((2,)),
            dma,
        ],
        compiler_params=pltpu.CompilerParams(
            collective_id=0, has_side_effects=True, vmem_limit_bytes=67043328
        ),
    )(parent_inverse.reshape(8, R, K), panel)
    return -product, saved_diag + gram


def solution(mesh):
    in_specs = (P("row", "col"), P(("col", "row"), None), P("row", "col"))
    out_specs = (P(("row", "col"), None), P("row", "col"))
    return jax.shard_map(shards, mesh=mesh, in_specs=in_specs, out_specs=out_specs, check_vma=False)
```

```python
import jax
import jax.numpy as jnp
from jax import lax
from jax.experimental import pallas as pl
from jax.experimental.pallas import tpu as pltpu
from jax.sharding import PartitionSpec as P

MESH = pl.DeviceIdType.MESH
F32 = jnp.float32
BF16 = jnp.bfloat16
CHUNKS = ((0, (0,)), (1, (0, 1)), (2, (0, 1)), (3, (0, 1)), (0, (1,)))
J = len(CHUNKS)
WIDTHS = tuple(128 * len(zls) for _, zls in CHUNKS)
H = 128
R = 192
K = 3072
SLAB = 256
SLABS = K // SLAB
STAGES = tuple(j for j in range(J) if WIDTHS[j] == SLAB)[:3]

ACROSS = ()

ORDER = (
    ("p0", 0), ("p0", 1), ("perm1",), ("p1a", 0), ("p2", 0), ("p1a", 1), ("sp", 4), ("sp", 5), ("p3", 0), ("p1b", 1),
    ("sp", 6), ("sp", 7), ("p2", 1), ("p1b", 0), ("sp", 8), ("sp", 9), ("p3", 1), ("p0", 2), ("sp", 10), ("sp", 11),
    ("p4b", 0), ("p4a", 0), ("p4c", 0), ("p0", 3), ("cv", 0), ("A", 0), ("BC", 0), ("p1a", 2), ("p4c", 1), ("p1b", 2),
    ("p4a", 1), ("p4b", 1), ("D", 0), ("r1", 0), ("cv", 1), ("p2", 2), ("p0", 4), ("A", 1), ("p1a", 3), ("p3", 2),
    ("p2", 3), ("r2", 0), ("BC", 1), ("p1b", 4), ("D", 1), ("p4c", 2), ("p1a", 4), ("p1b", 3), ("p4b", 2), ("p4a", 2),
    ("r3", 0), ("r1", 1), ("p3", 3), ("perm2",), ("cv", 2), ("A", 2), ("p2", 4), ("BC", 2), ("p4a", 3), ("p4c", 3),
    ("r2", 1), ("p4b", 3), ("p3", 4), ("D", 2), ("cv", 3), ("r1", 2), ("A", 3), ("BC", 3), ("r3", 1), ("r2", 2),
    ("take",), ("gr", 0), ("gr", 1), ("p4c", 4), ("r4", 0), ("r1", 3), ("p4a", 4), ("p4b", 4), ("r4", 1), ("D", 3),
    ("cv", 4), ("r3", 2), ("gr", 2), ("A", 4), ("r2", 3), ("r4", 2), ("BC", 4), ("r1", 4), ("D", 4), ("r5", 1),
    ("r3", 3), ("gr", 3), ("r2", 4), ("r4", 3), ("r6", 1), ("r5", 0), ("r3", 4), ("gr", 4), ("r5", 2), ("r4", 4),
    ("r5", 3), ("r5", 4), ("r6", 2), ("r6", 3), ("r6", 4), ("r6", 0),
)


def dot(a, b):
    return jnp.dot(a, b, preferred_element_type=F32)


def split(value):
    high = value.astype(BF16)
    return high, (value - high.astype(F32)).astype(BF16)


def kernel(*refs):
    pi, panel, out, diag, pih, pil, bh, bl, rows, mid, pth, ptl, fin = refs[:13]
    rest = refs[13:]
    gath, x1r, x2f, x2b, zrec, part, gp, gsr, a2a, fsend = (rest[i * J:(i + 1) * J] for i in range(10))
    (pisem, locsem, ag_s, ag_r, rs_s, rs_r, g_s, g_r, a_s, a_r, f_s, f_r,
     p1_s, p1_r, p2_s, p2_r) = rest[10 * J:]
    r, c = lax.axis_index("row"), lax.axis_index("col")
    zh, y, k = r // 8, (r // 2) % 4, r % 2
    zl, x = c // 4, c % 4
    z = zh * 2 + zl
    d = 1 - 2 * k

    def dev(z_, y_, x_, k_):
        return ((z_ // 2) * 8 + y_ * 2 + k_, (z_ % 2) * 4 + x_)

    def slot(zh_, y_, k_):
        return zh_ * 8 + y_ * 2 + k_

    yf, yb, y2 = (y + d + 4) % 4, (y - d + 4) % 4, (y + 2) % 4
    xf, xb, x2 = (x + d + 4) % 4, (x - d + 4) % 4, (x + 2) % 4
    zp, zt = zh * 2 + (1 - zl), (z + 2) % 4
    zo = 1 - zh
    sib = dev(z, y, x, 1 - k)
    to_yf, to_yb = dev(z, yf, x, k), dev(z, yb, x, k)
    to_zt, to_zp = dev(zt, y, x, k), dev(zp, y, x, k)
    to_xf, to_xb = dev(z, y, xf, k), dev(z, y, xb, k)

    def remote(src, dst, ss, rs, to):
        return pltpu.make_async_remote_copy(
            src_ref=src, dst_ref=dst, send_sem=ss, recv_sem=rs, device_id=to, device_id_type=MESH
        )

    def arrived(at, ss, rs):
        remote(at, at, ss, rs, sib).wait_recv()

    def sent(at, ss):
        remote(at, at, ss, p1_s, sib).wait_send()

    def columns(j, h):
        x_, zls = CHUNKS[j]
        return pl.ds((zls[h] * 4 + x_) * H, H)

    def own_copy(j, h):
        return pltpu.make_async_copy(
            panel.at[:, columns(j, h)], gath[j].at[r, :, pl.ds(h * H, H)], locsem.at[j, h]
        )

    def slab_copy(s):
        b = s % 3
        return pltpu.make_async_copy(pi.at[:, :, pl.ds(s * SLAB, SLAB)], part[STAGES[b]], pisem.at[b])

    for h in range(len(CHUNKS[0][1])):
        own_copy(0, h).start()
    for s in range(3):
        slab_copy(s).start()
    for j in range(1, J):
        for h in range(len(CHUNKS[j][1])):
            own_copy(j, h).start()

    barrier = pltpu.get_barrier_semaphore()
    peers = [to_yf, to_yb, to_zt, to_zp, sib]
    for dx in range(1, 4):
        for k_ in range(2):
            peers.append(dev(z, y, (x + dx) % 4, k_))
    for to in peers:
        pl.semaphore_signal(barrier, inc=1, device_id=to, device_id_type=MESH)

    def split_slab(s):
        b = part[STAGES[s % 3]]
        slab_copy(s).wait()

        def piece(q, carry):
            high, low = split(b[q])
            at = pl.ds(pl.multiple_of(((q % 4) * 2 + q // 4) * R, R), R)
            pih[at, s * SLAB:(s + 1) * SLAB] = high
            pil[at, s * SLAB:(s + 1) * SLAB] = low
            return carry

        lax.fori_loop(0, 8, piece, 0)
        if s + 3 < SLABS:
            slab_copy(s + 3).start()

    got = [slot(zh, yb, k), slot(zh, yf, k), slot(zo, y, k), None, slot(zo, yb, k), slot(zo, yf, k),
           slot(zh, y2, k), slot(zo, y2, k)]
    sib_slots = [slot(zh, y, k), got[0], got[1], got[2], got[6], got[4], got[5], got[7]]
    def ag(j, m):
        if m >= 8:
            source, to = sib_slots[m - 8], sib
        else:
            source = {0: r, 1: r, 2: r, 4: got[2], 5: got[2], 6: got[0], 7: got[6]}[m]
            to = {1: to_yb, 5: to_yb, 2: to_zt, 7: to_zt}.get(m, to_yf)
        at = gath[j].at[source]
        return remote(at, at, ag_s.at[j], ag_r.at[j, min(m, 8)], to)

    def ag_wait(j, m):
        at = gath[j].at[got[m]]
        arrived(at, ag_s.at[j], ag_r.at[j, m])

    def p0(j):
        for h in range(len(CHUNKS[j][1])):
            own_copy(j, h).wait()
        for m in (0, 2, 1, 8):
            ag(j, m).start()

    def relay(wait, *starts):
        def step(j):
            ag_wait(j, wait)
            for m in starts:
                ag(j, m).start()
        return step

    def cv(j):
        arrived(gath[j].at[0:8], ag_s.at[j], ag_r.at[j, 8])

        def body(q, carry):
            high, low = split(gath[j][q])
            at = pl.ds(pl.multiple_of(q * R, R), R)
            if WIDTHS[j] == H:
                bh[at, :H] = high
                bh[at, H:] = low
            else:
                bh[at, :] = high
                bl[at, :] = low
            return carry

        lax.fori_loop(0, 16, body, 0)

    def compute(j, pair):
        at = pl.ds(pl.multiple_of(pair * (2 * R), 2 * R), 2 * R)
        if WIDTHS[j] == H:
            wide = dot(pih[at, :], bh[...])
            total = wide[:, :H] + wide[:, H:] + dot(pil[at, :], bh[:, :H])
        else:
            total = dot(pih[at, :], bh[...]) + dot(pih[at, :], bl[...]) + dot(pil[at, :], bh[...])
        part[j][pl.ds(pair * 2, 2)] = total.reshape(2, R, WIDTHS[j])

    def rs(j, m):
        ss, rs_ = rs_s.at[j], rs_r.at[j, m]
        if m == 0 and j in ACROSS:
            return remote(part[j].at[x2 * 2 + zl], x1r[j].at[0], ss, rs_, to_xf)
        if m == 0:
            return remote(part[j].at[pl.ds(x2 * 2, 2)], x1r[j], ss, rs_, to_xf)
        if m == 4:
            return remote(part[j].at[x2 * 2 + (1 - zl)], x1r[j].at[1], ss, rs_, to_zp)
        if m == 1:
            return remote(part[j].at[pl.ds(xb * 2, 2)], x2b[j], ss, rs_, to_xb)
        if m == 2:
            return remote(part[j].at[pl.ds(xf * 2, 2)], x2f[j], ss, rs_, to_xf)
        return remote(part[j].at[x * 2 + (1 - zl)], zrec[j], ss, rs_, to_zp)

    def qa(j):
        compute(j, x2)
        rs(j, 4 if j in ACROSS else 0).start()

    def r0(j):
        rs(j, 4).wait_recv()
        part[j][x2 * 2 + zl] = part[j][x2 * 2 + zl] + x1r[j][1]
        rs(j, 0).start()

    def qbc(j):
        def body(i, carry):
            compute(j, jnp.where(i == 0, xb, xf))

            @pl.when(i == 0)
            def _():
                rs(j, 1).start()

            return carry

        lax.fori_loop(0, 2, body, 0)

    def qd(j):
        compute(j, x)

    def r1(j):
        rs(j, 0).wait_recv()
        if j in ACROSS:
            part[j][xf * 2 + zl] = part[j][xf * 2 + zl] + x1r[j][0]
        else:
            at = pl.ds(xf * 2, 2)
            part[j][at] = part[j][at] + x1r[j][...]
        rs(j, 2).start()

    def r2(j):
        rs(j, 1).wait_recv()
        rs(j, 2).wait_recv()
        q = 1 - zl
        part[j][x * 2 + q] = part[j][x * 2 + q] + x2f[j][q] + x2b[j][q]
        rs(j, 3).start()
        part[j][x * 2 + zl] = part[j][x * 2 + zl] + x2f[j][zl] + x2b[j][zl]

    def r3(j):
        rs(j, 3).wait_recv()
        product = part[j][x * 2 + zl] + zrec[j][...]
        part[j][x * 2 + zl] = product
        for h in range(len(CHUNKS[j][1])):
            out[:, columns(j, h)] = product[:, h * H:(h + 1) * H]

    def sib_gram(j):
        return remote(gp[j].at[:, 1 - k], gsr[j], g_s.at[j], g_r.at[j], sib)

    def gr(j):
        high, low = split(part[j][x * 2 + zl])
        for i in range(8):
            at = pl.ds(i * H, H)
            tile = dot(pth[at, :], high) + dot(pth[at, :], low) + dot(ptl[at, :], high)
            gp[j][i] = tile.reshape(2, 64, WIDTHS[j])
        sib_gram(j).start()

    def gram_to(j, i):
        zls = CHUNKS[j][1]
        if len(zls) == 2:
            z_ = (z + i // 4) % 4
            at = z_ % 2
        else:
            z_ = ((zh + i // 4) % 2) * 2 + zls[0]
            at = 0
        y_ = (y + i % 4) % 4
        source = gp[j].at[(z_ // 2) * 4 + y_, k, :, pl.ds(pl.multiple_of(at * H, H), H)]
        s = ((z_ - z + 4) % 4) * 4 + i % 4
        return remote(source, a2a[j].at[s], a_s.at[j], a_r.at[j], dev(z_, y_, x, k))

    def r4(j):
        arrived(gsr[j], g_s.at[j], g_r.at[j])
        for i in range(8):
            gp[j][i, k] = gp[j][i, k] + gsr[j][i]
        both = len(CHUNKS[j][1]) == 2
        for i in range(8 * len(CHUNKS[j][1])):
            if i or not both:
                copy = gram_to(j, i)
                copy.start() if i else pl.when(zl != CHUNKS[j][1][0])(copy.start)

    def takes(j, act):
        zls = CHUNKS[j][1]
        if len(zls) == 2:
            act()
        else:
            pl.when(zl == zls[0])(act)

    def last(j):
        x_ = CHUNKS[j][0]
        dx = (x - x_ + 4) % 4
        return remote(fsend[j], fin.at[dx], f_s.at[j], f_r.at[dx], dev(z, y, x_, k))

    def r5(j):
        def act():
            at = zl * H if len(CHUNKS[j][1]) == 2 else 0
            own = gp[j][zh * 4 + y, k, :, pl.ds(pl.multiple_of(at, H), H)]

            arrived(a2a[j].at[1:16], a_s.at[j], a_r.at[j])
            parts = [own] + [a2a[j][i] for i in range(1, 16)]
            while len(parts) > 1:
                parts = [a + b for a, b in zip(parts[::2], parts[1::2])]
            fsend[j][...] = parts[0]

            @pl.when(x != CHUNKS[j][0])
            def _():
                last(j).start()

        takes(j, act)

    def r6(j):
        def act():
            @pl.when(x == CHUNKS[j][0])
            def _():
                total = fsend[j][...]
                for dx in range(1, 4):
                    arrived(fin.at[dx], f_s.at[j], f_r.at[dx])
                    total = total + fin[dx]
                diag[...] = total

        takes(j, act)

    to_mid = dev(z, y, 2 * (y % 2) + k, x % 2)
    stays = jnp.logical_and(x == 2 * (y % 2) + k, x % 2 == k)
    is_mid = x // 2 == y % 2
    lands = jnp.logical_and(
        jnp.logical_and(y % 2 == k, zl == zh),
        jnp.logical_and(jnp.logical_and(y // 2 == zl, zh == k), is_mid),
    )
    perm1_copy = remote(panel, mid.at[x // 2], p1_s, p1_r.at[x // 2], to_mid)
    perm1_self = pltpu.make_async_copy(panel, mid.at[x // 2], p1_r.at[x // 2])

    def perm1():
        @pl.when(stays)
        def _():
            perm1_self.start()

        @pl.when(jnp.logical_not(stays))
        def _():
            perm1_copy.start()

    def perm2_copy(m):
        return remote(mid.at[m], rows, p2_s.at[m], p2_r, dev(2 * zl + y // 2, 2 * m + k, x, zh))

    def perm2_self(m):
        return pltpu.make_async_copy(mid.at[m], rows, p2_r)

    def perm2():
        @pl.when(is_mid)
        def _():
            for m in range(2):
                here = jnp.logical_and(stays, x // 2 == m)

                @pl.when(here)
                def _():
                    pltpu.make_async_copy(panel, mid.at[m], p1_r.at[m]).wait()

                @pl.when(jnp.logical_not(here))
                def _():
                    arrived(mid.at[m], p1_s, p1_r.at[m])

            for m in range(2):
                here = jnp.logical_and(lands, y // 2 == m)

                @pl.when(here)
                def _():
                    perm2_self(m).start()

                @pl.when(jnp.logical_not(here))
                def _():
                    perm2_copy(m).start()

    def take():
        @pl.when(lands)
        def _():
            perm2_self(0).wait()

        @pl.when(jnp.logical_not(lands))
        def _():
            arrived(rows, p2_s.at[0], p2_r)

        for i in range(8):
            high, low = split(rows[:, i * H:(i + 1) * H].T)
            pth[i * H:(i + 1) * H, :] = high
            ptl[i * H:(i + 1) * H, :] = low

    for s in range(4):
        split_slab(s)
    pl.semaphore_wait(barrier, len(peers))

    steps = {
        "sp": split_slab, "p0": p0, "p1a": relay(0, 6, 9), "p1b": relay(1, 10), "p2": relay(2, 4, 5, 11),
        "p3": relay(6, 7, 12), "p4a": relay(4, 13), "p4b": relay(5, 14), "p4c": relay(7, 15),
        "cv": cv, "A": qa, "BC": qbc, "D": qd, "r0": r0, "r1": r1, "r2": r2, "r3": r3, "gr": gr,
        "r4": r4, "r5": r5, "r6": r6, "perm1": perm1, "perm2": perm2, "take": take,
    }
    for step in ORDER:
        steps[step[0]](*step[1:])

    for j in range(J):
        sent(gath[j].at[0:15], ag_s.at[j])
        sent(gath[j].at[0:7], rs_s.at[j])
        sib_gram(j).wait_send()
        if len(CHUNKS[j][1]) == 2:
            sent(a2a[j].at[0:15], a_s.at[j])
        else:
            @pl.when(zl == CHUNKS[j][1][0])
            def _():
                sent(a2a[j].at[0:7], a_s.at[j])

            @pl.when(zl != CHUNKS[j][1][0])
            def _():
                sent(a2a[j].at[0:8], a_s.at[j])

        def final(j=j):
            @pl.when(x != CHUNKS[j][0])
            def _():
                last(j).wait_send()

        takes(j, final)

    @pl.when(jnp.logical_not(stays))
    def _():
        perm1_copy.wait_send()

    @pl.when(is_mid)
    def _():
        for m in range(2):
            @pl.when(jnp.logical_not(jnp.logical_and(lands, y // 2 == m)))
            def _():
                perm2_copy(m).wait_send()


def shards(parent_inverse, panel, saved_diag):
    vmem = pl.BlockSpec(memory_space=pltpu.VMEM)
    hbm = pl.BlockSpec(memory_space=pl.ANY)
    dma = pltpu.SemaphoreType.DMA

    def each(*shape):
        return [pltpu.VMEM(shape + (w,), F32) for w in WIDTHS]

    product, gram = pl.pallas_call(
        kernel,
        out_shape=(
            jax.ShapeDtypeStruct((R, 1024), F32),
            jax.ShapeDtypeStruct((64, H), F32),
        ),
        in_specs=[hbm, hbm],
        out_specs=(vmem, vmem),
        scratch_shapes=[
            pltpu.VMEM((8 * R, K), BF16),
            pltpu.VMEM((8 * R, K), BF16),
            pltpu.VMEM((K, max(WIDTHS)), BF16),
            pltpu.VMEM((K, max(WIDTHS)), BF16),
            pltpu.VMEM((R, 1024), F32),
            pltpu.VMEM((2, R, 1024), F32),
            pltpu.VMEM((1024, R), BF16),
            pltpu.VMEM((1024, R), BF16),
            pltpu.VMEM((4, 64, H), F32),
            *each(16, R),
            *each(2, R),
            *each(2, R),
            *each(2, R),
            *each(R),
            *each(8, R),
            *each(8, 2, 64),
            *each(8, 64),
            *[pltpu.VMEM((16, 64, H), F32) for _ in range(J)],
            *[pltpu.VMEM((64, H), F32) for _ in range(J)],
            dma((3,)),
            dma((J, 2)),
            dma((J,)),
            dma((J, 9)),
            dma((J,)),
            dma((J, 5)),
            dma((J,)),
            dma((J,)),
            dma((J,)),
            dma((J,)),
            dma((J,)),
            dma((4,)),
            dma,
            dma((2,)),
            dma((2,)),
            dma,
        ],
        compiler_params=pltpu.CompilerParams(
            collective_id=0, has_side_effects=True, vmem_limit_bytes=67043328
        ),
    )(parent_inverse.reshape(8, R, K), panel)
    return -product, saved_diag + gram


def solution(mesh):
    in_specs = (P("row", "col"), P(("col", "row"), None), P("row", "col"))
    out_specs = (P(("row", "col"), None), P("row", "col"))
    return jax.shard_map(shards, mesh=mesh, in_specs=in_specs, out_specs=out_specs, check_vma=False)
```
